32 devices in a mesh: mod: 8 (over z, y), mode: 4 (over x, core).
Axes of the slice: x: 2, y: 2, z: 4, core: 2. Of those that a mesh axis runs over, the one named last changes fastest.
Arguments:
- mod_points: int32 [8], P('mod'), may hold values from 0 to 47
- pupil_mask: int32 [256, 256], P('mode'), may hold values 0 or 1
- phase_offset: float32 [256, 256], P('mode'), may hold values from -6 to 6
- modes: bfloat16 [16, 256, 256], P('mode', 'mod'), may hold values from -6 to 6
- block_map: int32 [8], replicated, may hold values from 0 to 7, each once
Outputs:
- tangent: float32 [512, 16, 512], P('mod', 'mode')
The draws below stay inside these ranges and needn't reach their ends.
Inputs may be any that keep to these rules, and one draw needn't show every extreme that they name: `mod_points`: indices of points on a circle of 48 equally spaced modulation points; repeats are allowed. `block_map`: each of the 8 detector row blocks appears exactly once.
All inputs are finite; a program needn't handle non-finite values. No bound on the sum of `pupil_mask` on one device may be relied on, other than what follows from the above.
Results may differ from the reference program's by a relative error of at most 0.015.
Values may be sent and summed in bfloat16 or wider, within the bound.
A program may use at most 64 MiB of HBM per device.

```python
import math
import jax
import jax.numpy as jnp
from jax import lax

PUPIL = 256
PADDED = 512
NMODES = 16
MODS = 8
NPTS = 48
NBLK = 8


def place_ends(values, stream_key, least, high):
    place = [jax.random.randint(jax.random.fold_in(stream_key, axis), (), 0, length) for axis, length in enumerate(values.shape)]
    longest = values.shape.index(max(values.shape))
    neighbour = place[:longest] + [(place[longest] + 1) % values.shape[longest]] + place[longest + 1:]
    return values.at[tuple(place)].set(least).at[tuple(neighbour)].set(high)


def shard_levels(stream_key, dims, cuts, smallest, largest):
    gain = 1.0
    for dim, blocks in cuts:
        heights = jax.random.uniform(jax.random.fold_in(jax.random.fold_in(stream_key, 6), dim), (blocks,), jnp.float32, smallest / len(cuts), largest / len(cuts))
        gain = gain * jnp.repeat(jnp.exp(heights), dims[dim] // blocks).reshape((-1,) + (1,) * (len(dims) - 1 - dim))
    return gain


def normal_values(own_key, shape, spread, reach, pieces=(), kind=jnp.bfloat16):
    result = spread * jax.random.normal(own_key, shape, jnp.float32)
    if pieces:
        result = result * shard_levels(own_key, shape, pieces, -0.22, 0.18)
    return jnp.clip(result, -reach, reach).astype(kind)


def setup_inputs(seed: int = 0) -> dict:
    streams_of = jax.random.split(jax.random.key(seed), 6)
    return {
        "mod_points": place_ends(jax.random.randint(streams_of[0], (MODS,), 0, NPTS), jax.random.fold_in(streams_of[0], 1), 0, NPTS - 1).astype(jnp.int32),
        "pupil_mask": place_ends((jax.random.randint(streams_of[1], (PUPIL, PUPIL), 0, 8) < 7).astype(jnp.int32), jax.random.fold_in(streams_of[1], 1), 0, 1),
        "phase_offset": normal_values(streams_of[2], (PUPIL, PUPIL), 1.0, 6.0, ((0, 4),), jnp.float32),
        "modes": normal_values(streams_of[3], (NMODES, PUPIL, PUPIL), 1.0, 6.0, ((0, 4), (1, 8))),
        "block_map": jax.random.permutation(streams_of[4], NBLK).astype(jnp.int32),
    }


radius_cells = 6.0

def dft_table(left, right, length):
    turns = left[:, None] * right[None, :] % length
    angle = turns.astype(jnp.float32) * (2.0 * math.pi / length)
    norm = 1.0 / math.sqrt(length)
    return ((jnp.cos(angle) * norm).astype(jnp.bfloat16), (-jnp.sin(angle) * norm).astype(jnp.bfloat16))

def complex_product(form, left, right):
    left_re = left[0].astype(jnp.float32)
    left_im = left[1].astype(jnp.float32)
    right_re = right[0].astype(jnp.float32)
    right_im = right[1].astype(jnp.float32)
    high = lax.Precision.HIGHEST
    real = jnp.einsum(form, left_re, right_re, precision=high) - jnp.einsum(form, left_im, right_im, precision=high)
    imag = jnp.einsum(form, left_re, right_im, precision=high) + jnp.einsum(form, left_im, right_re, precision=high)
    return (real, imag)

def pyramid_parts(length):
    centred = jnp.arange(length, dtype=jnp.int32) - length // 2
    quarter = (jnp.abs(centred)[:, None] + jnp.abs(centred)[None, :]) % 4
    cos_part = (quarter == 0).astype(jnp.float32) - (quarter == 2).astype(jnp.float32)
    sin_part = (quarter == 1).astype(jnp.float32) - (quarter == 3).astype(jnp.float32)
    return (cos_part, sin_part)

def pupil_field(point, phase, mask):
    pupil = phase.shape[0]
    length = 2 * pupil
    theta = point.astype(jnp.float32) * (2.0 * math.pi / NPTS)
    centred = (jnp.arange(pupil, dtype=jnp.int32) - pupil // 2).astype(jnp.float32)
    tilt = 2.0 * math.pi * radius_cells / length * (jnp.cos(theta) * centred[:, None] + jnp.sin(theta) * centred[None, :])
    total = phase + tilt
    return ((mask * jnp.cos(total)).astype(jnp.bfloat16), (mask * jnp.sin(total)).astype(jnp.bfloat16))

def reference(mod_points, pupil_mask, phase_offset, modes, block_map):
    mask = pupil_mask.astype(jnp.float32)
    centred_pad = jnp.arange(PADDED, dtype=jnp.int32) - PADDED // 2
    centred_pupil = jnp.arange(PUPIL, dtype=jnp.int32) - PUPIL // 2
    first = dft_table(centred_pad, centred_pupil, PADDED)
    second = dft_table(centred_pad, centred_pad, PADDED)
    cos_part, sin_part = pyramid_parts(PADDED)
    values = modes.astype(jnp.float32)

    def one_point(total, point):
        field_re, field_im = pupil_field(point, phase_offset, mask)
        moved_re = (-values * field_im.astype(jnp.float32)).astype(jnp.bfloat16)
        moved_im = (values * field_re.astype(jnp.float32)).astype(jnp.bfloat16)
        all_re = jnp.concatenate([field_re[None], moved_re], axis=0)
        all_im = jnp.concatenate([field_im[None], moved_im], axis=0)
        a_re, a_im = complex_product('un,fnp->fup', first, (all_re, all_im))
        a_re = a_re.astype(jnp.bfloat16)
        a_im = a_im.astype(jnp.bfloat16)
        f_re, f_im = complex_product('fup,vp->fuv', (a_re, a_im), first)
        g_re = (cos_part * f_re - sin_part * f_im).astype(jnp.bfloat16)
        g_im = (cos_part * f_im + sin_part * f_re).astype(jnp.bfloat16)
        b_re, b_im = complex_product('um,fmv->fuv', second, (g_re, g_im))
        b_re = b_re.astype(jnp.bfloat16)
        b_im = b_im.astype(jnp.bfloat16)
        d_re, d_im = complex_product('fuv,pv->ufp', (b_re, b_im), second)
        term = 2.0 * (d_re[:, :1] * d_re[:, 1:] + d_im[:, :1] * d_im[:, 1:])
        return (total + term, None)
    start = jnp.zeros((PADDED, NMODES, PADDED), jnp.float32)
    summed = lax.scan(one_point, start, mod_points)[0]
    block_rows = PADDED // NBLK
    ordered = summed.reshape(NBLK, block_rows, NMODES, PADDED)[block_map].reshape(PADDED, NMODES, PADDED)
    return ordered * (float(PADDED * PADDED) / float(PUPIL * PUPIL * MODS))
```

```python
import functools
import math

import jax
import jax.numpy as jnp
import numpy as np
from jax import lax
from jax.experimental import pallas as pl
from jax.experimental.pallas import tpu as pltpu
from jax.sharding import PartitionSpec as P

NPTS = 48


radius_cells = 6.0


def operator_tables(pupil):
    length = 2 * pupil
    centred_pad = np.arange(length) - length // 2
    centred_pupil = np.arange(pupil) - pupil // 2
    first = np.exp(-2j * np.pi * (np.outer(centred_pad, centred_pupil) % length) / length)
    second = np.exp(-2j * np.pi * (np.outer(centred_pad, centred_pad) % length) / length)
    phasor = np.exp(0.5j * np.pi * (np.abs(centred_pad) % 4))
    whole = second @ (phasor[:, None] * first) / length
    mirror = (-np.arange(pupil)) % pupil
    hilbert = 2.0 * whole.imag[:pupil][mirror].T
    flip = np.zeros((pupil, pupil))
    flip[mirror, np.arange(pupil)] = 1.0
    return (
        whole.real.astype(np.float32),
        whole.imag.astype(np.float32),
        hilbert.astype(jnp.bfloat16),
        flip.astype(jnp.bfloat16),
    )


def tangent_kernel(
    factor, block_ref, points_ref, rows_re_ref, rows_im_ref, field_ref, modes_ref, hilbert_ref,
    flip_ref, out_ref, left_ref, weight_ref, rot_ref, bent_ref, wide_ref, own_ref, acc_ref,
):
    mods, pupil = points_ref.shape
    rows = rows_re_ref.shape[0]
    mode_dev = modes_ref.shape[0]
    f32 = jnp.float32
    bf16 = jnp.bfloat16
    theta = points_ref[...].astype(f32) * (2.0 * math.pi / NPTS)
    centred = (lax.broadcasted_iota(jnp.int32, (mods, pupil), 1) - pupil // 2).astype(f32)
    scale = 2.0 * math.pi * radius_cells / (2 * pupil)
    row_angle = scale * jnp.cos(theta) * centred
    col_angle = scale * jnp.sin(theta) * centred
    row_cos, row_sin = jnp.cos(row_angle), jnp.sin(row_angle)
    rot_ref[0] = jnp.cos(col_angle)
    rot_ref[1] = jnp.sin(col_angle)
    rows_re = rows_re_ref[...]
    rows_im = rows_im_ref[...]
    for k in range(mods):
        cos, sin = row_cos[k : k + 1], row_sin[k : k + 1]
        re = (rows_re * cos - rows_im * sin).astype(bf16)
        im = (rows_re * sin + rows_im * cos).astype(bf16)
        base = 2 * rows * k
        left_ref[base : base + rows, :pupil] = re
        left_ref[base : base + rows, pupil:] = -im
        left_ref[base + rows : base + 2 * rows, :pupil] = im
        left_ref[base + rows : base + 2 * rows, pupil:] = re

    def detector(own, mode):
        wide_ref[...] = jnp.dot(left_ref[...], weight_ref[...], preferred_element_type=f32)
        for k in range(mods):
            base = 2 * rows * k
            cos, sin = rot_ref[0, k : k + 1], rot_ref[1, k : k + 1]
            re = wide_ref[base : base + rows]
            im = wide_ref[base + rows : base + 2 * rows]
            turned_re = re * cos - im * sin
            turned_im = re * sin + im * cos
            wide_ref[base : base + rows] = turned_re
            wide_ref[base + rows : base + 2 * rows] = turned_im
            bent_ref[base : base + rows] = turned_re.astype(bf16)
            bent_ref[base + rows : base + 2 * rows] = turned_im.astype(bf16)
        side = jnp.dot(bent_ref[...], hilbert_ref[...], preferred_element_type=f32)
        total_low = total_high = None
        for k in range(mods):
            base = 2 * rows * k
            re = wide_ref[base : base + rows]
            im = wide_ref[base + rows : base + 2 * rows]
            side_re = side[base : base + rows]
            side_im = side[base + rows : base + 2 * rows]
            low_re, low_im = re - side_im, im + side_re
            high_re, high_im = re + side_im, im - side_re
            if own:
                own_ref[k, 0] = low_re
                own_ref[k, 1] = low_im
                own_ref[k, 2] = high_re
                own_ref[k, 3] = high_im
            else:
                low = own_ref[k, 0] * low_re + own_ref[k, 1] * low_im
                high = own_ref[k, 2] * high_re + own_ref[k, 3] * high_im
                total_low = low if total_low is None else total_low + low
                total_high = high if total_high is None else total_high + high
        if not own:
            for half, total in enumerate((total_low, total_high)):
                total = total * factor
                coarse = total.astype(bf16)
                fine = (total - coarse.astype(f32)).astype(bf16)
                placed = jnp.dot(coarse, flip_ref[...], preferred_element_type=f32) + jnp.dot(
                    fine, flip_ref[...], preferred_element_type=f32
                )
                out_ref[:, mode, half * pupil : (half + 1) * pupil] = placed

    weight_ref[:pupil] = field_ref[0]
    weight_ref[pupil:] = field_ref[1]
    detector(True, 0)
    for mode in range(mode_dev):
        values = modes_ref[mode].astype(f32)
        weight_ref[:pupil] = (-values * field_ref[1].astype(f32)).astype(bf16)
        weight_ref[pupil:] = (values * field_ref[0].astype(f32)).astype(bf16)
        detector(False, mode)


def tangent_call(block, points, field, modes, factor, rows, mods):
    mode_dev, pupil, _ = modes.shape
    rows_re, rows_im, hilbert, flip = operator_tables(pupil)
    whole = lambda *shape: pl.BlockSpec(shape, lambda i, b: (0,) * len(shape))
    picked = pl.BlockSpec((rows, pupil), lambda i, b: (b[0], 0))
    spec = pltpu.PrefetchScalarGridSpec(
        num_scalar_prefetch=1,
        grid=(1,),
        in_specs=[
            whole(mods, pupil),
            picked,
            picked,
            whole(2, pupil, pupil),
            whole(mode_dev, pupil, pupil),
            whole(pupil, pupil),
            whole(pupil, pupil),
        ],
        out_specs=whole(rows, mode_dev, 2 * pupil),
        scratch_shapes=[
            pltpu.VMEM((2 * rows * mods, 2 * pupil), jnp.bfloat16),
            pltpu.VMEM((2 * pupil, pupil), jnp.bfloat16),
            pltpu.VMEM((2, mods, pupil), jnp.float32),
            pltpu.VMEM((2 * rows * mods, pupil), jnp.bfloat16),
            pltpu.VMEM((2 * rows * mods, pupil), jnp.float32),
            pltpu.VMEM((mods, 4, rows, pupil), jnp.float32),
            pltpu.VMEM((rows, pupil), jnp.float32),
        ],
    )
    return pl.pallas_call(
        functools.partial(tangent_kernel, factor),
        grid_spec=spec,
        out_shape=jax.ShapeDtypeStruct((rows, mode_dev, 2 * pupil), jnp.float32),
        compiler_params=pltpu.CompilerParams(vmem_limit_bytes=48 * 1024 * 1024),
    )(block, points, rows_re, rows_im, field, modes, hilbert, flip)


def local(mod_points, pupil_mask, phase_offset, modes, block_map):
    mod_count = lax.axis_size("mod")
    mods = mod_points.shape[0] * mod_count
    pupil = modes.shape[2]
    length = 2 * pupil
    rows = length // block_map.shape[0]
    mask = pupil_mask.astype(jnp.float32)
    own = jnp.stack([mask * jnp.cos(phase_offset), mask * jnp.sin(phase_offset)])
    field = lax.all_gather(own.astype(jnp.bfloat16), "mode", axis=1, tiled=True)
    values = lax.all_gather(modes, "mod", axis=1, tiled=True)
    points = lax.all_gather(mod_points, "mod", axis=0, tiled=True)
    points = jnp.broadcast_to(points[:, None], (mods, pupil))
    block = lax.dynamic_slice(block_map, (lax.axis_index("mod"),), (1,))
    factor = 2.0 * 0.25 * float(length * length) / float(pupil * pupil * mods)
    return tangent_call(block, points, field, values, factor, rows, mods)


def solution(mesh):
    placed = (P("mod"), P("mode", None), P("mode", None), P("mode", "mod", None), P())
    return jax.shard_map(
        local, mesh=mesh, in_specs=placed, out_specs=P("mod", "mode", None), check_vma=False
    )
```

```python
import functools
import math

import jax
import jax.numpy as jnp
import numpy as np
from jax import lax
from jax.experimental import pallas as pl
from jax.experimental.pallas import tpu as pltpu
from jax.sharding import PartitionSpec as P

NPTS = 48


radius_cells = 6.0


def operator_tables(pupil):
    length = 2 * pupil
    centred_pad = np.arange(length) - length // 2
    centred_pupil = np.arange(pupil) - pupil // 2
    first = np.exp(-2j * np.pi * (np.outer(centred_pad, centred_pupil) % length) / length)
    second = np.exp(-2j * np.pi * (np.outer(centred_pad, centred_pad) % length) / length)
    phasor = np.exp(0.5j * np.pi * (np.abs(centred_pad) % 4))
    whole = second @ (phasor[:, None] * first) / length
    mirror = (-np.arange(pupil)) % pupil
    hilbert = 2.0 * whole.imag[:pupil][mirror].T
    flip = np.zeros((pupil, pupil))
    flip[mirror, np.arange(pupil)] = 1.0
    return (
        whole.imag[:pupil].astype(np.float32),
        hilbert.astype(jnp.bfloat16),
        flip.astype(jnp.bfloat16),
    )


def tangent_kernel(
    factor, blocks_ref, points_ref, rows_ref, field_ref, modes_ref, hilbert_ref, flip_ref, out_ref,
    left_ref, weight_ref, rot_ref, bent_ref, wide_ref, own_ref,
):
    mods = points_ref.shape[0]
    pupil = rows_ref.shape[0]
    rows = out_ref.shape[0]
    mode_dev = modes_ref.shape[0]
    f32 = jnp.float32
    bf16 = jnp.bfloat16
    theta = points_ref[...][:, 0, :1].astype(f32) * (2.0 * math.pi / NPTS)
    centred = (lax.broadcasted_iota(jnp.int32, (mods, pupil), 1) - pupil // 2).astype(f32)
    scale = 2.0 * math.pi * radius_cells / (2 * pupil)
    row_angle = scale * jnp.cos(theta) * centred
    col_angle = scale * jnp.sin(theta) * centred
    row_cos, row_sin = jnp.cos(row_angle), jnp.sin(row_angle)
    rot_ref[0] = jnp.cos(col_angle)
    rot_ref[1] = jnp.sin(col_angle)
    start = blocks_ref[lax.axis_index("mod")] * rows
    sign = jnp.where(start < pupil, 1.0, -1.0).astype(f32)
    start = lax.rem(start, pupil)
    rows_im = sign * rows_ref[pl.ds(pl.multiple_of(start, rows), rows), :]
    facing = lax.rem(
        start
        + lax.broadcasted_iota(jnp.int32, (rows, pupil), 0)
        + lax.broadcasted_iota(jnp.int32, (rows, pupil), 1),
        pupil,
    )
    rows_re = jnp.where(facing == 0, 0.5, 0.0).astype(f32)
    for k in range(mods):
        cos, sin = row_cos[k : k + 1], row_sin[k : k + 1]
        re = (rows_re * cos - rows_im * sin).astype(bf16)
        im = (rows_re * sin + rows_im * cos).astype(bf16)
        base = 2 * rows * k
        left_ref[base : base + rows, :pupil] = re
        left_ref[base : base + rows, pupil:] = -im
        left_ref[base + rows : base + 2 * rows, :pupil] = im
        left_ref[base + rows : base + 2 * rows, pupil:] = re

    def detector(own, mode):
        wide_ref[...] = jnp.dot(left_ref[...], weight_ref[...], preferred_element_type=f32)
        for k in range(mods):
            base = 2 * rows * k
            cos, sin = rot_ref[0, k : k + 1], rot_ref[1, k : k + 1]
            re = wide_ref[base : base + rows]
            im = wide_ref[base + rows : base + 2 * rows]
            turned_re = re * cos - im * sin
            turned_im = re * sin + im * cos
            wide_ref[base : base + rows] = turned_re
            wide_ref[base + rows : base + 2 * rows] = turned_im
            bent_ref[base : base + rows] = turned_re.astype(bf16)
            bent_ref[base + rows : base + 2 * rows] = turned_im.astype(bf16)
        side = jnp.dot(bent_ref[...], hilbert_ref[...], preferred_element_type=f32)
        total_low = total_high = None
        for k in range(mods):
            base = 2 * rows * k
            re = wide_ref[base : base + rows]
            im = wide_ref[base + rows : base + 2 * rows]
            side_re = side[base : base + rows]
            side_im = side[base + rows : base + 2 * rows]
            low_re, low_im = re - side_im, im + side_re
            high_re, high_im = re + side_im, im - side_re
            if own:
                own_ref[k, 0] = low_re
                own_ref[k, 1] = low_im
                own_ref[k, 2] = high_re
                own_ref[k, 3] = high_im
            else:
                low = own_ref[k, 0] * low_re + own_ref[k, 1] * low_im
                high = own_ref[k, 2] * high_re + own_ref[k, 3] * high_im
                total_low = low if total_low is None else total_low + low
                total_high = high if total_high is None else total_high + high
        if not own:
            for half, total in enumerate((total_low, total_high)):
                total = total * factor
                coarse = total.astype(bf16)
                fine = (total - coarse.astype(f32)).astype(bf16)
                placed = jnp.dot(coarse, flip_ref[...], preferred_element_type=f32) + jnp.dot(
                    fine, flip_ref[...], preferred_element_type=f32
                )
                out_ref[:, mode, half * pupil : (half + 1) * pupil] = placed

    weight_ref[:pupil] = field_ref[0]
    weight_ref[pupil:] = field_ref[1]
    detector(True, 0)
    for mode in range(mode_dev):
        values = modes_ref[mode].astype(f32)
        weight_ref[:pupil] = (-values * field_ref[1].astype(f32)).astype(bf16)
        weight_ref[pupil:] = (values * field_ref[0].astype(f32)).astype(bf16)
        detector(False, mode)


def gather_kernel(
    count_y, point_ref, mask_ref, phase_ref, modes_ref, points_ref, field_ref, values_ref,
    own_point, own_field, local_sem, point_send, point_recv, field_send, field_recv, z_send,
    z_recv, y_send, y_recv,
):
    mod_count = lax.axis_size("mod")
    mode_count = lax.axis_size("mode")
    count_z = mod_count // count_y
    me, mine = lax.axis_index("mod"), lax.axis_index("mode")
    y, z = lax.rem(me, count_y), me // count_y
    mode_dev, share, pupil = modes_ref.shape
    stripe = mask_ref.shape[0]
    mesh = pl.DeviceIdType.MESH
    along_z = [lax.rem(z + d, count_z) * count_y + y for d in range(1, count_z)]
    from_z = [lax.rem(z + count_z - d, count_z) * count_y + y for d in range(1, count_z)]
    along_y = [z * count_y + lax.rem(y + d, count_y) for d in range(1, count_y)]
    beside = [lax.rem(mine + d, mode_count) for d in range(1, mode_count)]

    barrier = pltpu.get_barrier_semaphore()
    for peer in along_z + along_y:
        pl.semaphore_signal(barrier, inc=1, device_id=(peer, mine), device_id_type=mesh)
    for peer in beside:
        pl.semaphore_signal(barrier, inc=1, device_id=(me, peer), device_id_type=mesh)

    own_point[...] = jnp.full(own_point.shape, point_ref[0], jnp.int32)
    mask = mask_ref[...].astype(jnp.float32)
    own_field[0] = (mask * jnp.cos(phase_ref[...])).astype(jnp.bfloat16)
    own_field[1] = (mask * jnp.sin(phase_ref[...])).astype(jnp.bfloat16)
    pl.semaphore_wait(barrier, len(along_z) + len(along_y) + len(beside))

    def lines(i):
        return pl.ds(pl.multiple_of(i * share, share), share)

    def send(source, target, sent, landed, peer):
        copy = pltpu.make_async_remote_copy(
            src_ref=source, dst_ref=target, send_sem=sent, recv_sem=landed,
            device_id=peer, device_id_type=mesh,
        )
        copy.start()
        return copy

    copies = []
    for d, peer in enumerate(along_z):
        copies.append(
            send(own_point, points_ref.at[me], point_send.at[d], point_recv.at[d], (peer, mine))
        )
    for d, peer in enumerate(along_y):
        copies.append(
            send(
                own_point, points_ref.at[me], point_send.at[count_z - 1 + d],
                point_recv.at[count_z - 1 + d], (peer, mine),
            )
        )
    held = pl.ds(pl.multiple_of(mine * stripe, stripe), stripe)
    field_copies = [
        send(own_field, field_ref.at[:, held], field_send.at[d], field_recv.at[d], (me, peer))
        for d, peer in enumerate(beside)
    ]
    z_copies = []
    y_copies = []
    for j in range(mode_dev):
        here = values_ref.at[j, lines(me)]
        z_copies.append([
            send(modes_ref.at[j], here, z_send.at[j, d], z_recv.at[j, d], (peer, mine))
            for d, peer in enumerate(along_z)
        ])
        y_copies.append([
            send(modes_ref.at[j], here, y_send.at[j, 0, d], y_recv.at[j, 0, d], (peer, mine))
            for d, peer in enumerate(along_y)
        ])
    stay = [
        pltpu.make_async_copy(own_point, points_ref.at[me], local_sem.at[0]),
        pltpu.make_async_copy(own_field, field_ref.at[:, held], local_sem.at[1]),
        pltpu.make_async_copy(modes_ref, values_ref.at[:, lines(me)], local_sem.at[2]),
    ]
    for copy in stay:
        copy.start()

    for d, source in enumerate(from_z):
        copies[d].wait_recv()
        for e, peer in enumerate(along_y):
            at = count_z - 1 + (d + 1) * len(along_y) + e
            copies.append(
                send(
                    points_ref.at[source], points_ref.at[source], point_send.at[at],
                    point_recv.at[at], (peer, mine),
                )
            )
    for j in range(mode_dev):
        for d, source in enumerate(from_z):
            z_copies[j][d].wait_recv()
            piece = values_ref.at[j, lines(source)]
            for e, peer in enumerate(along_y):
                y_copies[j].append(
                    send(piece, piece, y_send.at[j, d + 1, e], y_recv.at[j, d + 1, e], (peer, mine))
                )
    for copy in stay:
        copy.wait()
    for copy in copies[count_z - 1 :]:
        copy.wait_recv()
    for copy in field_copies:
        copy.wait_recv()
    for j in range(mode_dev):
        for copy in y_copies[j]:
            copy.wait_recv()
    for copy in copies + field_copies + sum(z_copies, []) + sum(y_copies, []):
        copy.wait_send()


def gather_call(mod_points, pupil_mask, phase_offset, modes):
    mod_count = lax.axis_size("mod")
    mode_count = lax.axis_size("mode")
    mode_dev, share, pupil = modes.shape
    count_y = 2 if mod_count % 2 == 0 else 1
    count_z = mod_count // count_y
    vmem = pl.BlockSpec(memory_space=pltpu.VMEM)
    dma = pltpu.SemaphoreType.DMA
    few = max(count_y - 1, 1)
    points = count_z - 1 + count_z * few
    return pl.pallas_call(
        functools.partial(gather_kernel, count_y),
        in_specs=[pl.BlockSpec(memory_space=pltpu.SMEM), vmem, vmem, vmem],
        out_specs=(vmem, vmem, vmem),
        out_shape=(
            jax.ShapeDtypeStruct((mod_count, 8, 128), jnp.int32),
            jax.ShapeDtypeStruct((2, pupil, pupil), jnp.bfloat16),
            jax.ShapeDtypeStruct((mode_dev, pupil, pupil), jnp.bfloat16),
        ),
        scratch_shapes=[
            pltpu.VMEM((8, 128), jnp.int32),
            pltpu.VMEM((2, pupil_mask.shape[0], pupil), jnp.bfloat16),
            dma((3,)),
            dma((points,)),
            dma((points,)),
            dma((mode_count - 1,)),
            dma((mode_count - 1,)),
            dma((mode_dev, count_z - 1)),
            dma((mode_dev, count_z - 1)),
            dma((mode_dev, count_z, few)),
            dma((mode_dev, count_z, few)),
        ],
        compiler_params=pltpu.CompilerParams(collective_id=0, has_side_effects=True),
    )(mod_points, pupil_mask, phase_offset, modes)


def tangent_call(block_map, points, field, modes, factor, rows, mods):
    mode_dev, pupil, _ = modes.shape
    below, hilbert, flip = operator_tables(pupil)
    vmem = pl.BlockSpec(memory_space=pltpu.VMEM)
    return pl.pallas_call(
        functools.partial(tangent_kernel, factor),
        in_specs=[pl.BlockSpec(memory_space=pltpu.SMEM)] + [vmem] * 6,
        out_specs=vmem,
        scratch_shapes=[
            pltpu.VMEM((2 * rows * mods, 2 * pupil), jnp.bfloat16),
            pltpu.VMEM((2 * pupil, pupil), jnp.bfloat16),
            pltpu.VMEM((2, mods, pupil), jnp.float32),
            pltpu.VMEM((2 * rows * mods, pupil), jnp.bfloat16),
            pltpu.VMEM((2 * rows * mods, pupil), jnp.float32),
            pltpu.VMEM((mods, 4, rows, pupil), jnp.float32),
        ],
        out_shape=jax.ShapeDtypeStruct((rows, mode_dev, 2 * pupil), jnp.float32),
        compiler_params=pltpu.CompilerParams(vmem_limit_bytes=48 * 1024 * 1024),
    )(block_map, points, below, field, modes, hilbert, flip)


def local(mod_points, pupil_mask, phase_offset, modes, block_map):
    mod_count = lax.axis_size("mod")
    mods = mod_points.shape[0] * mod_count
    pupil = modes.shape[2]
    length = 2 * pupil
    rows = length // block_map.shape[0]
    points, field, values = gather_call(mod_points, pupil_mask, phase_offset, modes)
    factor = 2.0 * 0.25 * float(length * length) / float(pupil * pupil * mods)
    return tangent_call(block_map, points, field, values, factor, rows, mods)


def solution(mesh):
    placed = (P("mod"), P("mode", None), P("mode", None), P("mode", "mod", None), P())
    return jax.shard_map(
        local, mesh=mesh, in_specs=placed, out_specs=P("mod", "mode", None), check_vma=False
    )
```

```python
import functools
import math

import jax
import jax.numpy as jnp
import numpy as np
from jax import lax
from jax.experimental import pallas as pl
from jax.experimental.pallas import tpu as pltpu
from jax.sharding import PartitionSpec as P

NPTS = 48


radius_cells = 6.0


def operator_tables(pupil):
    length = 2 * pupil
    centred_pad = np.arange(length) - length // 2
    centred_pupil = np.arange(pupil) - pupil // 2
    first = np.exp(-2j * np.pi * (np.outer(centred_pad, centred_pupil) % length) / length)
    second = np.exp(-2j * np.pi * (np.outer(centred_pad, centred_pad) % length) / length)
    phasor = np.exp(0.5j * np.pi * (np.abs(centred_pad) % 4))
    whole = second @ (phasor[:, None] * first) / length
    mirror = (-np.arange(pupil)) % pupil
    hilbert = 2.0 * whole.imag[:pupil][mirror].T
    flip = np.zeros((pupil, pupil))
    flip[mirror, np.arange(pupil)] = 1.0
    return (
        whole.imag[:pupil].astype(np.float32),
        hilbert.astype(jnp.bfloat16),
        flip.astype(jnp.bfloat16),
    )


def tangent_kernel(
    factor, count_y, point_ref, blocks_ref, mask_hbm, phase_hbm, modes_hbm, rows_hbm, hilbert_hbm,
    flip_hbm, out_ref, points_ref, field_ref, values_ref, own_point, own_field, mask_ref, phase_ref,
    rows_ref, hilbert_ref, flip_ref, left_ref, weight_ref, rot_ref, bent_ref, wide_ref, own_ref,
    local_sem, point_send, point_recv, field_send, field_recv, z_send, z_recv, relay_send, y_send,
    y_recv,
):
    mod_count = lax.axis_size("mod")
    mode_count = lax.axis_size("mode")
    count_z = mod_count // count_y
    me, mine = lax.axis_index("mod"), lax.axis_index("mode")
    y, z = lax.rem(me, count_y), me // count_y
    mode_dev, share, pupil = modes_hbm.shape
    stripe = mask_ref.shape[0]
    mods = mod_count
    rows = out_ref.shape[0]
    f32 = jnp.float32
    bf16 = jnp.bfloat16
    mesh = pl.DeviceIdType.MESH
    along_z = [lax.rem(z + d, count_z) * count_y + y for d in range(1, count_z)]
    from_z = [lax.rem(z + count_z - d, count_z) * count_y + y for d in range(1, count_z)]
    along_y = [z * count_y + lax.rem(y + d, count_y) for d in range(1, count_y)]
    beside = [lax.rem(mine + d, mode_count) for d in range(1, mode_count)]
    relayed = count_z == 4

    early = [
        pltpu.make_async_copy(mask_hbm, mask_ref, local_sem.at[0]),
        pltpu.make_async_copy(phase_hbm, phase_ref, local_sem.at[1]),
    ]
    tables = [
        pltpu.make_async_copy(rows_hbm, rows_ref, local_sem.at[2]),
        pltpu.make_async_copy(hilbert_hbm, hilbert_ref, local_sem.at[3]),
        pltpu.make_async_copy(flip_hbm, flip_ref, local_sem.at[4]),
    ]
    barrier = pltpu.get_barrier_semaphore()
    for peer in along_z + along_y:
        pl.semaphore_signal(barrier, inc=1, device_id=(peer, mine), device_id_type=mesh)
    for peer in beside:
        pl.semaphore_signal(barrier, inc=1, device_id=(me, peer), device_id_type=mesh)
    for copy in early + tables:
        copy.start()

    own_point[...] = jnp.full(own_point.shape, point_ref[0], jnp.int32)
    for copy in early:
        copy.wait()
    mask = mask_ref[...].astype(f32)
    own_field[0] = (mask * jnp.cos(phase_ref[...])).astype(bf16)
    own_field[1] = (mask * jnp.sin(phase_ref[...])).astype(bf16)
    pl.semaphore_wait(barrier, len(along_z) + len(along_y) + len(beside))

    def lines(i):
        return pl.ds(pl.multiple_of(i * share, share), share)

    def make(source, target, sent, landed, peer):
        return pltpu.make_async_remote_copy(
            src_ref=source, dst_ref=target, send_sem=sent, recv_sem=landed,
            device_id=peer, device_id_type=mesh,
        )

    def send(*args):
        copy = make(*args)
        copy.start()
        return copy

    copies = []
    for d, peer in enumerate(along_z):
        copies.append(
            send(own_point, points_ref.at[me], point_send.at[d], point_recv.at[d], (peer, mine))
        )
    for d, peer in enumerate(along_y):
        copies.append(
            send(
                own_point, points_ref.at[me], point_send.at[count_z - 1 + d],
                point_recv.at[count_z - 1 + d], (peer, mine),
            )
        )
    held = pl.ds(pl.multiple_of(mine * stripe, stripe), stripe)
    field_copies = [
        send(own_field, field_ref.at[:, held], field_send.at[d], field_recv.at[d], (me, peer))
        for d, peer in enumerate(beside)
    ]

    def ends(d):
        if not relayed or d == 1:
            return None
        return count_z - 1 if d == 0 else 0

    order = [1, 0, 2] if relayed else list(range(count_z - 1))
    z_copies = []
    y_copies = []
    relays = []
    for j in range(mode_dev):
        here = values_ref.at[j, lines(me)]
        row = [
            make(modes_hbm.at[j], here, z_send.at[j, d], z_recv.at[j, d], (peer, mine))
            for d, peer in enumerate(along_z)
        ]
        for d in order:
            if ends(d) is None:
                row[d].start()
            else:
                pl.when(z != ends(d))(row[d].start)
        z_copies.append(row)
        y_copies.append([
            send(modes_hbm.at[j], here, y_send.at[j, 0, d], y_recv.at[j, 0, d], (peer, mine))
            for d, peer in enumerate(along_y)
        ])
        if relayed:
            piece = values_ref.at[j, lines(from_z[1])]
            relays.append([
                make(piece, piece, relay_send.at[j], z_recv.at[j, 0], (y, mine)),
                make(piece, piece, relay_send.at[j], z_recv.at[j, 2], (3 * count_y + y, mine)),
            ])
    stay = [
        pltpu.make_async_copy(own_point, points_ref.at[me], local_sem.at[5]),
        pltpu.make_async_copy(own_field, field_ref.at[:, held], local_sem.at[6]),
        pltpu.make_async_copy(modes_hbm, values_ref.at[:, lines(me)], local_sem.at[7]),
    ]
    for copy in stay:
        copy.start()

    for d, source in enumerate(from_z):
        copies[d].wait_recv()
        for e, peer in enumerate(along_y):
            at = count_z - 1 + (d + 1) * len(along_y) + e
            copies.append(
                send(
                    points_ref.at[source], points_ref.at[source], point_send.at[at],
                    point_recv.at[at], (peer, mine),
                )
            )

    def forward(j):
        for d in order:
            z_copies[j][d].wait_recv()
            if relayed and d == 1:
                pl.when(z == 1)(relays[j][0].start)
                pl.when(z == 2)(relays[j][1].start)
            piece = values_ref.at[j, lines(from_z[d])]
            for e, peer in enumerate(along_y):
                y_copies[j].append(
                    send(piece, piece, y_send.at[j, d + 1, e], y_recv.at[j, d + 1, e], (peer, mine))
                )

    for copy in tables + stay:
        copy.wait()
    for copy in copies[count_z - 1 :]:
        copy.wait_recv()
    theta = points_ref[...][:, 0, :1].astype(f32) * (2.0 * math.pi / NPTS)
    centred = (lax.broadcasted_iota(jnp.int32, (mods, pupil), 1) - pupil // 2).astype(f32)
    scale = 2.0 * math.pi * radius_cells / (2 * pupil)
    row_angle = scale * jnp.cos(theta) * centred
    col_angle = scale * jnp.sin(theta) * centred
    row_cos, row_sin = jnp.cos(row_angle), jnp.sin(row_angle)
    rot_ref[0] = jnp.cos(col_angle)
    rot_ref[1] = jnp.sin(col_angle)
    block = blocks_ref[me]
    place = lax.broadcasted_iota(jnp.int32, (rows, pupil), 0) + lax.broadcasted_iota(
        jnp.int32, (rows, pupil), 1
    )
    rows_re = jnp.zeros((rows, pupil), f32)
    rows_im = jnp.zeros((rows, pupil), f32)
    for b in range(blocks_ref.shape[0]):
        chosen = (jnp.full((1, pupil), block, jnp.int32) == b).astype(f32)
        start = b * rows % pupil
        facing = ((place + start) % pupil == 0).astype(f32)
        sign = 1.0 if b * rows < pupil else -1.0
        rows_re += 0.5 * chosen * facing
        rows_im += sign * chosen * rows_ref[start : start + rows]
    for k in range(mods):
        cos, sin = row_cos[k : k + 1], row_sin[k : k + 1]
        re = (rows_re * cos - rows_im * sin).astype(bf16)
        im = (rows_re * sin + rows_im * cos).astype(bf16)
        base = 2 * rows * k
        left_ref[base : base + rows, :pupil] = re
        left_ref[base : base + rows, pupil:] = -im
        left_ref[base + rows : base + 2 * rows, :pupil] = im
        left_ref[base + rows : base + 2 * rows, pupil:] = re

    def detector(own, mode):
        wide_ref[...] = jnp.dot(left_ref[...], weight_ref[...], preferred_element_type=f32)
        for k in range(mods):
            base = 2 * rows * k
            cos, sin = rot_ref[0, k : k + 1], rot_ref[1, k : k + 1]
            re = wide_ref[base : base + rows]
            im = wide_ref[base + rows : base + 2 * rows]
            turned_re = re * cos - im * sin
            turned_im = re * sin + im * cos
            wide_ref[base : base + rows] = turned_re
            wide_ref[base + rows : base + 2 * rows] = turned_im
            bent_ref[base : base + rows] = turned_re.astype(bf16)
            bent_ref[base + rows : base + 2 * rows] = turned_im.astype(bf16)
        side = jnp.dot(bent_ref[...], hilbert_ref[...], preferred_element_type=f32)
        total_low = total_high = None
        for k in range(mods):
            base = 2 * rows * k
            re = wide_ref[base : base + rows]
            im = wide_ref[base + rows : base + 2 * rows]
            side_re = side[base : base + rows]
            side_im = side[base + rows : base + 2 * rows]
            low_re, low_im = re - side_im, im + side_re
            high_re, high_im = re + side_im, im - side_re
            if own:
                own_ref[k, 0] = low_re
                own_ref[k, 1] = low_im
                own_ref[k, 2] = high_re
                own_ref[k, 3] = high_im
            else:
                low = own_ref[k, 0] * low_re + own_ref[k, 1] * low_im
                high = own_ref[k, 2] * high_re + own_ref[k, 3] * high_im
                total_low = low if total_low is None else total_low + low
                total_high = high if total_high is None else total_high + high
        if not own:
            for half, total in enumerate((total_low, total_high)):
                total = total * factor
                coarse = total.astype(bf16)
                fine = (total - coarse.astype(f32)).astype(bf16)
                placed = jnp.dot(coarse, flip_ref[...], preferred_element_type=f32) + jnp.dot(
                    fine, flip_ref[...], preferred_element_type=f32
                )
                out_ref[:, mode, half * pupil : (half + 1) * pupil] = placed

    forward(0)
    if mode_dev > 1:
        forward(1)
    for copy in field_copies:
        copy.wait_recv()
    weight_ref[:pupil] = field_ref[0]
    weight_ref[pupil:] = field_ref[1]
    detector(True, 0)
    for mode in range(2, mode_dev):
        forward(mode)
    for mode in range(mode_dev):
        for copy in y_copies[mode]:
            copy.wait_recv()
        values = values_ref[mode].astype(f32)
        weight_ref[:pupil] = (-values * field_ref[1].astype(f32)).astype(bf16)
        weight_ref[pupil:] = (values * field_ref[0].astype(f32)).astype(bf16)
        detector(False, mode)
    for copy in copies + field_copies + sum(y_copies, []):
        copy.wait_send()
    for j in range(mode_dev):
        for d in range(count_z - 1):
            if ends(d) is None:
                z_copies[j][d].wait_send()
            else:
                pl.when(z != ends(d))(z_copies[j][d].wait_send)
        if relayed:
            pl.when(z == 1)(relays[j][0].wait_send)
            pl.when(z == 2)(relays[j][1].wait_send)


def tangent_call(mod_points, pupil_mask, phase_offset, modes, block_map, factor):
    mod_count = lax.axis_size("mod")
    mode_count = lax.axis_size("mode")
    mode_dev, share, pupil = modes.shape
    stripe = pupil_mask.shape[0]
    rows = 2 * pupil // block_map.shape[0]
    count_y = 2 if mod_count % 2 == 0 else 1
    count_z = mod_count // count_y
    below, hilbert, flip = operator_tables(pupil)
    smem = pl.BlockSpec(memory_space=pltpu.SMEM)
    away = pl.BlockSpec(memory_space=pl.ANY)
    dma = pltpu.SemaphoreType.DMA
    few = max(count_y - 1, 1)
    points = count_z - 1 + count_z * few
    tall = 2 * rows * mod_count
    bf16 = jnp.bfloat16
    f32 = jnp.float32
    return pl.pallas_call(
        functools.partial(tangent_kernel, factor, count_y),
        in_specs=[smem, smem] + [away] * 6,
        out_specs=pl.BlockSpec(memory_space=pltpu.VMEM),
        out_shape=jax.ShapeDtypeStruct((rows, mode_dev, 2 * pupil), f32),
        scratch_shapes=[
            pltpu.VMEM((mod_count, 8, 128), jnp.int32),
            pltpu.VMEM((2, pupil, pupil), bf16),
            pltpu.VMEM((mode_dev, pupil, pupil), bf16),
            pltpu.VMEM((8, 128), jnp.int32),
            pltpu.VMEM((2, stripe, pupil), bf16),
            pltpu.VMEM((stripe, pupil), jnp.int32),
            pltpu.VMEM((stripe, pupil), f32),
            pltpu.VMEM((pupil, pupil), f32),
            pltpu.VMEM((pupil, pupil), bf16),
            pltpu.VMEM((pupil, pupil), bf16),
            pltpu.VMEM((tall, 2 * pupil), bf16),
            pltpu.VMEM((2 * pupil, pupil), bf16),
            pltpu.VMEM((2, mod_count, pupil), f32),
            pltpu.VMEM((tall, pupil), bf16),
            pltpu.VMEM((tall, pupil), f32),
            pltpu.VMEM((mod_count, 4, rows, pupil), f32),
            dma((8,)),
            dma((points,)),
            dma((points,)),
            dma((mode_count - 1,)),
            dma((mode_count - 1,)),
            dma((mode_dev, count_z - 1)),
            dma((mode_dev, count_z - 1)),
            dma((mode_dev,)),
            dma((mode_dev, count_z, few)),
            dma((mode_dev, count_z, few)),
        ],
        compiler_params=pltpu.CompilerParams(
            collective_id=0, has_side_effects=True, vmem_limit_bytes=60 * 1024 * 1024
        ),
    )(mod_points, block_map, pupil_mask, phase_offset, modes, below, hilbert, flip)


def local(mod_points, pupil_mask, phase_offset, modes, block_map):
    mods = mod_points.shape[0] * lax.axis_size("mod")
    pupil = modes.shape[2]
    length = 2 * pupil
    factor = 2.0 * 0.25 * float(length * length) / float(pupil * pupil * mods)
    return tangent_call(mod_points, pupil_mask, phase_offset, modes, block_map, factor)


def solution(mesh):
    placed = (P("mod"), P("mode", None), P("mode", None), P("mode", "mod", None), P())
    return jax.shard_map(
        local, mesh=mesh, in_specs=placed, out_specs=P("mod", "mode", None), check_vma=False
    )
```

```python
import functools
import math

import jax
import jax.numpy as jnp
import numpy as np
from jax import lax
from jax.experimental import pallas as pl
from jax.experimental.pallas import tpu as pltpu
from jax.sharding import PartitionSpec as P

NPTS = 48


radius_cells = 6.0


def operator_tables(pupil):
    length = 2 * pupil
    centred_pad = np.arange(length) - length // 2
    centred_pupil = np.arange(pupil) - pupil // 2
    first = np.exp(-2j * np.pi * (np.outer(centred_pad, centred_pupil) % length) / length)
    second = np.exp(-2j * np.pi * (np.outer(centred_pad, centred_pad) % length) / length)
    phasor = np.exp(0.5j * np.pi * (np.abs(centred_pad) % 4))
    whole = second @ (phasor[:, None] * first) / length
    mirror = (-np.arange(pupil)) % pupil
    hilbert = 2.0 * whole.imag[:pupil][mirror].T
    flip = np.zeros((pupil, pupil))
    flip[mirror, np.arange(pupil)] = 1.0
    return (
        whole.imag[:pupil].astype(np.float32),
        hilbert.astype(jnp.bfloat16),
        flip.astype(jnp.bfloat16),
    )


def tangent_kernel(
    factor, count_y, point_ref, blocks_ref, mask_hbm, phase_hbm, modes_hbm, rows_hbm, hilbert_hbm,
    flip_hbm, out_ref, points_ref, field_ref, values_ref, own_point, own_field, mask_ref, phase_ref,
    rows_ref, hilbert_ref, flip_ref, left_ref, weight_ref, rot_ref, bent_ref, wide_ref, own_ref,
    local_sem, point_send, point_recv, field_send, field_recv, z_send, z_recv, y_send,
    y_recv,
):
    mod_count = lax.axis_size("mod")
    mode_count = lax.axis_size("mode")
    count_z = mod_count // count_y
    me, mine = lax.axis_index("mod"), lax.axis_index("mode")
    y, z = lax.rem(me, count_y), me // count_y
    mode_dev, share, pupil = modes_hbm.shape
    stripe = mask_ref.shape[0]
    mods = mod_count
    rows = out_ref.shape[0]
    f32 = jnp.float32
    bf16 = jnp.bfloat16
    mesh = pl.DeviceIdType.MESH
    along_z = [lax.rem(z + d, count_z) * count_y + y for d in range(1, count_z)]
    from_z = [lax.rem(z + count_z - d, count_z) * count_y + y for d in range(1, count_z)]
    along_y = [z * count_y + lax.rem(y + d, count_y) for d in range(1, count_y)]
    beside = [lax.rem(mine + d, mode_count) for d in range(1, mode_count)]

    early = [
        pltpu.make_async_copy(mask_hbm, mask_ref, local_sem.at[0]),
        pltpu.make_async_copy(phase_hbm, phase_ref, local_sem.at[1]),
    ]
    tables = [
        pltpu.make_async_copy(rows_hbm, rows_ref, local_sem.at[2]),
        pltpu.make_async_copy(hilbert_hbm, hilbert_ref, local_sem.at[3]),
        pltpu.make_async_copy(flip_hbm, flip_ref, local_sem.at[4]),
    ]
    barrier = pltpu.get_barrier_semaphore()
    for peer in along_z + along_y:
        pl.semaphore_signal(barrier, inc=1, device_id=(peer, mine), device_id_type=mesh)
    for peer in beside:
        pl.semaphore_signal(barrier, inc=1, device_id=(me, peer), device_id_type=mesh)
    for copy in early + tables:
        copy.start()

    own_point[...] = jnp.full(own_point.shape, point_ref[0], jnp.int32)
    for copy in early:
        copy.wait()
    mask = mask_ref[...].astype(f32)
    own_field[0] = (mask * jnp.cos(phase_ref[...])).astype(bf16)
    own_field[1] = (mask * jnp.sin(phase_ref[...])).astype(bf16)
    pl.semaphore_wait(barrier, len(along_z) + len(along_y) + len(beside))

    def lines(i):
        return pl.ds(pl.multiple_of(i * share, share), share)

    def send(source, target, sent, landed, peer):
        copy = pltpu.make_async_remote_copy(
            src_ref=source, dst_ref=target, send_sem=sent, recv_sem=landed,
            device_id=peer, device_id_type=mesh,
        )
        copy.start()
        return copy

    copies = []
    for d, peer in enumerate(along_z):
        copies.append(
            send(own_point, points_ref.at[me], point_send.at[d], point_recv.at[d], (peer, mine))
        )
    for d, peer in enumerate(along_y):
        copies.append(
            send(
                own_point, points_ref.at[me], point_send.at[count_z - 1 + d],
                point_recv.at[count_z - 1 + d], (peer, mine),
            )
        )
    held = pl.ds(pl.multiple_of(mine * stripe, stripe), stripe)
    field_copies = [
        send(own_field, field_ref.at[:, held], field_send.at[d], field_recv.at[d], (me, peer))
        for d, peer in enumerate(beside)
    ]

    z_copies = []
    y_copies = []
    for j in range(mode_dev):
        here = values_ref.at[j, lines(me)]
        z_copies.append([
            send(modes_hbm.at[j], here, z_send.at[j, d], z_recv.at[j, d], (peer, mine))
            for d, peer in enumerate(along_z)
        ])
        y_copies.append([
            send(modes_hbm.at[j], here, y_send.at[j, 0, d], y_recv.at[j, 0, d], (peer, mine))
            for d, peer in enumerate(along_y)
        ])
    stay = [
        pltpu.make_async_copy(own_point, points_ref.at[me], local_sem.at[5]),
        pltpu.make_async_copy(own_field, field_ref.at[:, held], local_sem.at[6]),
        pltpu.make_async_copy(modes_hbm, values_ref.at[:, lines(me)], local_sem.at[7]),
    ]
    for copy in stay:
        copy.start()

    for d, source in enumerate(from_z):
        copies[d].wait_recv()
        for e, peer in enumerate(along_y):
            at = count_z - 1 + (d + 1) * len(along_y) + e
            copies.append(
                send(
                    points_ref.at[source], points_ref.at[source], point_send.at[at],
                    point_recv.at[at], (peer, mine),
                )
            )

    def forward(j):
        for d in range(count_z - 1):
            z_copies[j][d].wait_recv()
            piece = values_ref.at[j, lines(from_z[d])]
            for e, peer in enumerate(along_y):
                y_copies[j].append(
                    send(piece, piece, y_send.at[j, d + 1, e], y_recv.at[j, d + 1, e], (peer, mine))
                )

    for copy in tables + stay:
        copy.wait()
    for copy in copies[count_z - 1 :]:
        copy.wait_recv()
    theta = points_ref[...][:, 0, :1].astype(f32) * (2.0 * math.pi / NPTS)
    centred = (lax.broadcasted_iota(jnp.int32, (mods, pupil), 1) - pupil // 2).astype(f32)
    scale = 2.0 * math.pi * radius_cells / (2 * pupil)
    row_angle = scale * jnp.cos(theta) * centred
    col_angle = scale * jnp.sin(theta) * centred
    row_cos, row_sin = jnp.cos(row_angle), jnp.sin(row_angle)
    rot_ref[0] = jnp.cos(col_angle)
    rot_ref[1] = jnp.sin(col_angle)
    block = blocks_ref[me]
    place = lax.broadcasted_iota(jnp.int32, (rows, pupil), 0) + lax.broadcasted_iota(
        jnp.int32, (rows, pupil), 1
    )
    rows_re = jnp.zeros((rows, pupil), f32)
    rows_im = jnp.zeros((rows, pupil), f32)
    for b in range(blocks_ref.shape[0]):
        chosen = (jnp.full((1, pupil), block, jnp.int32) == b).astype(f32)
        start = b * rows % pupil
        facing = ((place + start) % pupil == 0).astype(f32)
        sign = 1.0 if b * rows < pupil else -1.0
        rows_re += 0.5 * chosen * facing
        rows_im += sign * chosen * rows_ref[start : start + rows]
    for k in range(mods):
        cos, sin = row_cos[k : k + 1], row_sin[k : k + 1]
        re = (rows_re * cos - rows_im * sin).astype(bf16)
        im = (rows_re * sin + rows_im * cos).astype(bf16)
        base = 2 * rows * k
        left_ref[base : base + rows, :pupil] = re
        left_ref[base : base + rows, pupil:] = -im
        left_ref[base + rows : base + 2 * rows, :pupil] = im
        left_ref[base + rows : base + 2 * rows, pupil:] = re

    def detector(own, mode):
        wide_ref[...] = jnp.dot(left_ref[...], weight_ref[...], preferred_element_type=f32)
        for k in range(mods):
            base = 2 * rows * k
            cos, sin = rot_ref[0, k : k + 1], rot_ref[1, k : k + 1]
            re = wide_ref[base : base + rows]
            im = wide_ref[base + rows : base + 2 * rows]
            turned_re = re * cos - im * sin
            turned_im = re * sin + im * cos
            wide_ref[base : base + rows] = turned_re
            wide_ref[base + rows : base + 2 * rows] = turned_im
            bent_ref[base : base + rows] = turned_re.astype(bf16)
            bent_ref[base + rows : base + 2 * rows] = turned_im.astype(bf16)
        side = jnp.dot(bent_ref[...], hilbert_ref[...], preferred_element_type=f32)
        total_low = total_high = None
        for k in range(mods):
            base = 2 * rows * k
            re = wide_ref[base : base + rows]
            im = wide_ref[base + rows : base + 2 * rows]
            side_re = side[base : base + rows]
            side_im = side[base + rows : base + 2 * rows]
            low_re, low_im = re - side_im, im + side_re
            high_re, high_im = re + side_im, im - side_re
            if own:
                own_ref[k, 0] = low_re
                own_ref[k, 1] = low_im
                own_ref[k, 2] = high_re
                own_ref[k, 3] = high_im
            else:
                low = own_ref[k, 0] * low_re + own_ref[k, 1] * low_im
                high = own_ref[k, 2] * high_re + own_ref[k, 3] * high_im
                total_low = low if total_low is None else total_low + low
                total_high = high if total_high is None else total_high + high
        if not own:
            for half, total in enumerate((total_low, total_high)):
                total = total * factor
                coarse = total.astype(bf16)
                fine = (total - coarse.astype(f32)).astype(bf16)
                placed = jnp.dot(coarse, flip_ref[...], preferred_element_type=f32) + jnp.dot(
                    fine, flip_ref[...], preferred_element_type=f32
                )
                out_ref[:, mode, half * pupil : (half + 1) * pupil] = placed

    forward(0)
    if mode_dev > 1:
        forward(1)
    for copy in field_copies:
        copy.wait_recv()
    weight_ref[:pupil] = field_ref[0]
    weight_ref[pupil:] = field_ref[1]
    detector(True, 0)
    for mode in range(2, mode_dev):
        forward(mode)
    for mode in range(mode_dev):
        for copy in y_copies[mode]:
            copy.wait_recv()
        values = values_ref[mode].astype(f32)
        weight_ref[:pupil] = (-values * field_ref[1].astype(f32)).astype(bf16)
        weight_ref[pupil:] = (values * field_ref[0].astype(f32)).astype(bf16)
        detector(False, mode)
    for copy in copies + field_copies + sum(z_copies, []) + sum(y_copies, []):
        copy.wait_send()


def tangent_call(mod_points, pupil_mask, phase_offset, modes, block_map, factor):
    mod_count = lax.axis_size("mod")
    mode_count = lax.axis_size("mode")
    mode_dev, share, pupil = modes.shape
    stripe = pupil_mask.shape[0]
    rows = 2 * pupil // block_map.shape[0]
    count_y = 2 if mod_count % 2 == 0 else 1
    count_z = mod_count // count_y
    below, hilbert, flip = operator_tables(pupil)
    smem = pl.BlockSpec(memory_space=pltpu.SMEM)
    away = pl.BlockSpec(memory_space=pl.ANY)
    dma = pltpu.SemaphoreType.DMA
    few = max(count_y - 1, 1)
    points = count_z - 1 + count_z * few
    tall = 2 * rows * mod_count
    bf16 = jnp.bfloat16
    f32 = jnp.float32
    return pl.pallas_call(
        functools.partial(tangent_kernel, factor, count_y),
        in_specs=[smem, smem] + [away] * 6,
        out_specs=pl.BlockSpec(memory_space=pltpu.VMEM),
        out_shape=jax.ShapeDtypeStruct((rows, mode_dev, 2 * pupil), f32),
        scratch_shapes=[
            pltpu.VMEM((mod_count, 8, 128), jnp.int32),
            pltpu.VMEM((2, pupil, pupil), bf16),
            pltpu.VMEM((mode_dev, pupil, pupil), bf16),
            pltpu.VMEM((8, 128), jnp.int32),
            pltpu.VMEM((2, stripe, pupil), bf16),
            pltpu.VMEM((stripe, pupil), jnp.int32),
            pltpu.VMEM((stripe, pupil), f32),
            pltpu.VMEM((pupil, pupil), f32),
            pltpu.VMEM((pupil, pupil), bf16),
            pltpu.VMEM((pupil, pupil), bf16),
            pltpu.VMEM((tall, 2 * pupil), bf16),
            pltpu.VMEM((2 * pupil, pupil), bf16),
            pltpu.VMEM((2, mod_count, pupil), f32),
            pltpu.VMEM((tall, pupil), bf16),
            pltpu.VMEM((tall, pupil), f32),
            pltpu.VMEM((mod_count, 4, rows, pupil), f32),
            dma((8,)),
            dma((points,)),
            dma((points,)),
            dma((mode_count - 1,)),
            dma((mode_count - 1,)),
            dma((mode_dev, count_z - 1)),
            dma((mode_dev, count_z - 1)),
            dma((mode_dev, count_z, few)),
            dma((mode_dev, count_z, few)),
        ],
        compiler_params=pltpu.CompilerParams(
            collective_id=0, has_side_effects=True, vmem_limit_bytes=60 * 1024 * 1024
        ),
    )(mod_points, block_map, pupil_mask, phase_offset, modes, below, hilbert, flip)


def local(mod_points, pupil_mask, phase_offset, modes, block_map):
    mods = mod_points.shape[0] * lax.axis_size("mod")
    pupil = modes.shape[2]
    length = 2 * pupil
    factor = 2.0 * 0.25 * float(length * length) / float(pupil * pupil * mods)
    return tangent_call(mod_points, pupil_mask, phase_offset, modes, block_map, factor)


def solution(mesh):
    placed = (P("mod"), P("mode", None), P("mode", None), P("mode", "mod", None), P())
    return jax.shard_map(
        local, mesh=mesh, in_specs=placed, out_specs=P("mod", "mode", None), check_vma=False
    )
```

```python
import functools
import math

import jax
import jax.numpy as jnp
import numpy as np
from jax import lax
from jax.experimental import pallas as pl
from jax.experimental.pallas import tpu as pltpu
from jax.sharding import PartitionSpec as P

NPTS = 48


radius_cells = 6.0


def operator_tables(pupil):
    length = 2 * pupil
    centred_pad = np.arange(length) - length // 2
    centred_pupil = np.arange(pupil) - pupil // 2
    first = np.exp(-2j * np.pi * (np.outer(centred_pad, centred_pupil) % length) / length)
    second = np.exp(-2j * np.pi * (np.outer(centred_pad, centred_pad) % length) / length)
    phasor = np.exp(0.5j * np.pi * (np.abs(centred_pad) % 4))
    whole = second @ (phasor[:, None] * first) / length
    mirror = (-np.arange(pupil)) % pupil
    hilbert = 2.0 * whole.imag[:pupil][mirror].T
    flip = np.zeros((pupil, pupil))
    flip[mirror, np.arange(pupil)] = 1.0
    return (
        whole.imag[:pupil].astype(np.float32),
        hilbert.astype(jnp.bfloat16),
        flip.astype(jnp.bfloat16),
    )


def tangent_kernel(
    factor, count_y, point_ref, blocks_ref, mask_hbm, phase_hbm, modes_hbm, rows_hbm, hilbert_hbm,
    out_ref, points_ref, field_ref, values_ref, own_point, own_field, mask_ref, phase_ref,
    rows_ref, hilbert_ref, left_ref, weight_ref, rot_ref, bent_ref, wide_ref, own_ref,
    local_sem, point_send, point_recv, field_send, field_recv, z_send, z_recv, y_send,
    y_recv,
):
    mod_count = lax.axis_size("mod")
    mode_count = lax.axis_size("mode")
    count_z = mod_count // count_y
    me, mine = lax.axis_index("mod"), lax.axis_index("mode")
    y, z = lax.rem(me, count_y), me // count_y
    mode_dev, share, pupil = modes_hbm.shape
    stripe = mask_ref.shape[0]
    mods = mod_count
    rows = out_ref.shape[3]
    f32 = jnp.float32
    bf16 = jnp.bfloat16
    mesh = pl.DeviceIdType.MESH
    along_z = [lax.rem(z + d, count_z) * count_y + y for d in range(1, count_z)]
    from_z = [lax.rem(z + count_z - d, count_z) * count_y + y for d in range(1, count_z)]
    along_y = [z * count_y + lax.rem(y + d, count_y) for d in range(1, count_y)]
    beside = [lax.rem(mine + d, mode_count) for d in range(1, mode_count)]

    early = [
        pltpu.make_async_copy(mask_hbm, mask_ref, local_sem.at[0]),
        pltpu.make_async_copy(phase_hbm, phase_ref, local_sem.at[1]),
    ]
    tables = [
        pltpu.make_async_copy(rows_hbm, rows_ref, local_sem.at[2]),
        pltpu.make_async_copy(hilbert_hbm, hilbert_ref, local_sem.at[3]),
    ]
    barrier = pltpu.get_barrier_semaphore()
    for peer in along_z + along_y:
        pl.semaphore_signal(barrier, inc=1, device_id=(peer, mine), device_id_type=mesh)
    for peer in beside:
        pl.semaphore_signal(barrier, inc=1, device_id=(me, peer), device_id_type=mesh)
    for copy in early + tables:
        copy.start()

    own_point[...] = jnp.full(own_point.shape, point_ref[0], jnp.int32)
    for copy in early:
        copy.wait()
    mask = mask_ref[...].astype(f32)
    own_field[0] = (mask * jnp.cos(phase_ref[...])).astype(bf16)
    own_field[1] = (mask * jnp.sin(phase_ref[...])).astype(bf16)
    pl.semaphore_wait(barrier, len(along_z) + len(along_y) + len(beside))

    def lines(i):
        return pl.ds(pl.multiple_of(i * share, share), share)

    def send(source, target, sent, landed, peer):
        copy = pltpu.make_async_remote_copy(
            src_ref=source, dst_ref=target, send_sem=sent, recv_sem=landed,
            device_id=peer, device_id_type=mesh,
        )
        copy.start()
        return copy

    copies = []
    for d, peer in enumerate(along_z):
        copies.append(
            send(own_point, points_ref.at[me], point_send.at[d], point_recv.at[d], (peer, mine))
        )
    for d, peer in enumerate(along_y):
        copies.append(
            send(
                own_point, points_ref.at[me], point_send.at[count_z - 1 + d],
                point_recv.at[count_z - 1 + d], (peer, mine),
            )
        )
    held = pl.ds(pl.multiple_of(mine * stripe, stripe), stripe)
    field_copies = [
        send(own_field, field_ref.at[:, held], field_send.at[d], field_recv.at[d], (me, peer))
        for d, peer in enumerate(beside)
    ]

    z_copies = []
    y_copies = []
    for j in range(mode_dev):
        here = values_ref.at[j, lines(me)]
        z_copies.append([
            send(modes_hbm.at[j], here, z_send.at[j, d], z_recv.at[j, d], (peer, mine))
            for d, peer in enumerate(along_z)
        ])
        y_copies.append([
            send(modes_hbm.at[j], here, y_send.at[j, 0, d], y_recv.at[j, 0, d], (peer, mine))
            for d, peer in enumerate(along_y)
        ])
    stay = [
        pltpu.make_async_copy(own_point, points_ref.at[me], local_sem.at[5]),
        pltpu.make_async_copy(own_field, field_ref.at[:, held], local_sem.at[6]),
        pltpu.make_async_copy(modes_hbm, values_ref.at[:, lines(me)], local_sem.at[7]),
    ]
    for copy in stay:
        copy.start()

    for d, source in enumerate(from_z):
        copies[d].wait_recv()
        for e, peer in enumerate(along_y):
            at = count_z - 1 + (d + 1) * len(along_y) + e
            copies.append(
                send(
                    points_ref.at[source], points_ref.at[source], point_send.at[at],
                    point_recv.at[at], (peer, mine),
                )
            )

    def forward(j):
        for d in range(count_z - 1):
            z_copies[j][d].wait_recv()
            piece = values_ref.at[j, lines(from_z[d])]
            for e, peer in enumerate(along_y):
                y_copies[j].append(
                    send(piece, piece, y_send.at[j, d + 1, e], y_recv.at[j, d + 1, e], (peer, mine))
                )

    for copy in tables + stay:
        copy.wait()
    for copy in copies[count_z - 1 :]:
        copy.wait_recv()
    theta = points_ref[...][:, 0, :1].astype(f32) * (2.0 * math.pi / NPTS)
    centred = (lax.broadcasted_iota(jnp.int32, (mods, pupil), 1) - pupil // 2).astype(f32)
    scale = 2.0 * math.pi * radius_cells / (2 * pupil)
    row_angle = scale * jnp.cos(theta) * centred
    col_angle = scale * jnp.sin(theta) * centred
    row_cos, row_sin = jnp.cos(row_angle), jnp.sin(row_angle)
    rot_ref[0] = jnp.cos(col_angle)
    rot_ref[1] = jnp.sin(col_angle)
    block = blocks_ref[me]
    place = lax.broadcasted_iota(jnp.int32, (rows, pupil), 0) + lax.broadcasted_iota(
        jnp.int32, (rows, pupil), 1
    )
    rows_re = jnp.zeros((rows, pupil), f32)
    rows_im = jnp.zeros((rows, pupil), f32)
    for b in range(blocks_ref.shape[0]):
        chosen = (jnp.full((1, pupil), block, jnp.int32) == b).astype(f32)
        start = b * rows % pupil
        facing = ((place + start) % pupil == 0).astype(f32)
        sign = 1.0 if b * rows < pupil else -1.0
        rows_re += 0.5 * chosen * facing
        rows_im += sign * chosen * rows_ref[start : start + rows]
    for k in range(mods):
        cos, sin = row_cos[k : k + 1], row_sin[k : k + 1]
        re = (rows_re * cos - rows_im * sin).astype(bf16)
        im = (rows_re * sin + rows_im * cos).astype(bf16)
        base = 2 * rows * k
        left_ref[base : base + rows, :pupil] = re
        left_ref[base : base + rows, pupil:] = -im
        left_ref[base + rows : base + 2 * rows, :pupil] = im
        left_ref[base + rows : base + 2 * rows, pupil:] = re

    def detector(own, mode):
        wide_ref[...] = jnp.dot(left_ref[...], weight_ref[...], preferred_element_type=f32)
        for k in range(mods):
            base = 2 * rows * k
            cos, sin = rot_ref[0, k : k + 1], rot_ref[1, k : k + 1]
            re = wide_ref[base : base + rows]
            im = wide_ref[base + rows : base + 2 * rows]
            turned_re = re * cos - im * sin
            turned_im = re * sin + im * cos
            wide_ref[base : base + rows] = turned_re
            wide_ref[base + rows : base + 2 * rows] = turned_im
            bent_ref[base : base + rows] = turned_re.astype(bf16)
            bent_ref[base + rows : base + 2 * rows] = turned_im.astype(bf16)
        side = jnp.dot(bent_ref[...], hilbert_ref[...], preferred_element_type=f32)
        total_low = total_high = None
        for k in range(mods):
            base = 2 * rows * k
            re = wide_ref[base : base + rows]
            im = wide_ref[base + rows : base + 2 * rows]
            side_re = side[base : base + rows]
            side_im = side[base + rows : base + 2 * rows]
            low_re, low_im = re - side_im, im + side_re
            high_re, high_im = re + side_im, im - side_re
            if own:
                own_ref[k, 0] = low_re
                own_ref[k, 1] = low_im
                own_ref[k, 2] = high_re
                own_ref[k, 3] = high_im
            else:
                low = own_ref[k, 0] * low_re + own_ref[k, 1] * low_im
                high = own_ref[k, 2] * high_re + own_ref[k, 3] * high_im
                total_low = low if total_low is None else total_low + low
                total_high = high if total_high is None else total_high + high
        if not own:
            for half, total in enumerate((total_low, total_high)):
                total = total * factor
                coarse = total.astype(bf16)
                fine = (total - coarse.astype(f32)).astype(bf16)
                out_ref[mode, 0, half] = coarse
                out_ref[mode, 1, half] = fine

    forward(0)
    if mode_dev > 1:
        forward(1)
    for copy in field_copies:
        copy.wait_recv()
    weight_ref[:pupil] = field_ref[0]
    weight_ref[pupil:] = field_ref[1]
    detector(True, 0)
    for mode in range(2, mode_dev):
        forward(mode)
    for mode in range(mode_dev):
        for copy in y_copies[mode]:
            copy.wait_recv()
        values = values_ref[mode].astype(f32)
        weight_ref[:pupil] = (-values * field_ref[1].astype(f32)).astype(bf16)
        weight_ref[pupil:] = (values * field_ref[0].astype(f32)).astype(bf16)
        detector(False, mode)
    for copy in copies + field_copies + sum(z_copies, []) + sum(y_copies, []):
        copy.wait_send()


def tangent_call(mod_points, pupil_mask, phase_offset, modes, block_map, factor):
    mod_count = lax.axis_size("mod")
    mode_count = lax.axis_size("mode")
    mode_dev, share, pupil = modes.shape
    stripe = pupil_mask.shape[0]
    rows = 2 * pupil // block_map.shape[0]
    count_y = 2 if mod_count % 2 == 0 else 1
    count_z = mod_count // count_y
    below, hilbert, _ = operator_tables(pupil)
    smem = pl.BlockSpec(memory_space=pltpu.SMEM)
    away = pl.BlockSpec(memory_space=pl.ANY)
    dma = pltpu.SemaphoreType.DMA
    few = max(count_y - 1, 1)
    points = count_z - 1 + count_z * few
    tall = 2 * rows * mod_count
    bf16 = jnp.bfloat16
    f32 = jnp.float32
    return pl.pallas_call(
        functools.partial(tangent_kernel, factor, count_y),
        in_specs=[smem, smem] + [away] * 5,
        out_specs=pl.BlockSpec(memory_space=pltpu.VMEM),
        out_shape=jax.ShapeDtypeStruct((mode_dev, 2, 2, rows, pupil), bf16),
        scratch_shapes=[
            pltpu.VMEM((mod_count, 8, 128), jnp.int32),
            pltpu.VMEM((2, pupil, pupil), bf16),
            pltpu.VMEM((mode_dev, pupil, pupil), bf16),
            pltpu.VMEM((8, 128), jnp.int32),
            pltpu.VMEM((2, stripe, pupil), bf16),
            pltpu.VMEM((stripe, pupil), jnp.int32),
            pltpu.VMEM((stripe, pupil), f32),
            pltpu.VMEM((pupil, pupil), f32),
            pltpu.VMEM((pupil, pupil), bf16),
            pltpu.VMEM((tall, 2 * pupil), bf16),
            pltpu.VMEM((2 * pupil, pupil), bf16),
            pltpu.VMEM((2, mod_count, pupil), f32),
            pltpu.VMEM((tall, pupil), bf16),
            pltpu.VMEM((tall, pupil), f32),
            pltpu.VMEM((mod_count, 4, rows, pupil), f32),
            dma((8,)),
            dma((points,)),
            dma((points,)),
            dma((mode_count - 1,)),
            dma((mode_count - 1,)),
            dma((mode_dev, count_z - 1)),
            dma((mode_dev, count_z - 1)),
            dma((mode_dev, count_z, few)),
            dma((mode_dev, count_z, few)),
        ],
        compiler_params=pltpu.CompilerParams(
            collective_id=0, has_side_effects=True, vmem_limit_bytes=60 * 1024 * 1024
        ),
    )(mod_points, block_map, pupil_mask, phase_offset, modes, below, hilbert)


def mirror_kernel(parts_ref, flip_ref, out_ref):
    mode_dev, _, halves, _, pupil = parts_ref.shape
    for mode in range(mode_dev):
        for half in range(halves):
            coarse = jnp.dot(
                parts_ref[mode, 0, half], flip_ref[...], preferred_element_type=jnp.float32
            )
            fine = jnp.dot(
                parts_ref[mode, 1, half], flip_ref[...], preferred_element_type=jnp.float32
            )
            out_ref[:, mode, half * pupil : (half + 1) * pupil] = coarse + fine


def mirror_call(parts):
    mode_dev, _, halves, rows, pupil = parts.shape
    flip = operator_tables(pupil)[2]
    vmem = pl.BlockSpec(memory_space=pltpu.VMEM)
    return pl.pallas_call(
        mirror_kernel,
        in_specs=[vmem, vmem],
        out_specs=vmem,
        out_shape=jax.ShapeDtypeStruct((rows, mode_dev, halves * pupil), jnp.float32),
    )(parts, flip)


def local(mod_points, pupil_mask, phase_offset, modes, block_map):
    mods = mod_points.shape[0] * lax.axis_size("mod")
    pupil = modes.shape[2]
    length = 2 * pupil
    factor = 2.0 * 0.25 * float(length * length) / float(pupil * pupil * mods)
    parts = tangent_call(mod_points, pupil_mask, phase_offset, modes, block_map, factor)
    return mirror_call(parts)


def solution(mesh):
    placed = (P("mod"), P("mode", None), P("mode", None), P("mode", "mod", None), P())
    return jax.shard_map(
        local, mesh=mesh, in_specs=placed, out_specs=P("mod", "mode", None), check_vma=False
    )
```
